32 devices in a mesh: ang: 4 (over y, x), rad: 8 (over z, core).
Axes of the slice: x: 2, y: 2, z: 4, core: 2. Of those that a mesh axis runs over, the one named last changes fastest.
Arguments:
- right_side: float32 [1024, 4096], P('rad', 'ang'), may hold values from -6 to 7
- guess: float32 [1024, 4096], P('rad', 'ang'), may hold values from -6 to 6
Outputs:
- solution: float32 [1024, 4096], P('rad', 'ang')
- residual: float32 [1024, 4096], P('rad', 'ang')
The draws below stay inside these ranges and needn't reach their ends.
All inputs are finite; a program needn't handle non-finite values.
Results may differ from the reference program's by a relative error of at most 0.007.
Values sent between devices are 32-bit elements; how exact they have to be, the bound alone decides.
No kernel may reach another device: no remote copies, remote signals or barrier semaphores. Data moves between devices by JAX's collectives and lax.ppermute only.
A program may use at most 128 MiB of HBM per device.

```python
import math
import jax
import jax.numpy as jnp

LEVELS = 8
PRE = 2
POST = 2
COARSE_SWEEPS = 8
NR = 1024
NT = 4096


def draw_right_side(key, part):
    rough_part = jnp.clip(jax.random.normal(key, (NR, NT), jnp.float32), -6.0, 6.0)
    return rough_part


def levels(key, dims, cuts, low, top_value):
    gain, own = 1.0, jax.random.fold_in(key, 6)
    for position, blocks in cuts:
        steps = jnp.exp(jax.random.uniform(jax.random.fold_in(own, position), (blocks,), jnp.float32, low / len(cuts), top_value / len(cuts)))
        gain = gain * jnp.repeat(steps, dims[position] // blocks).reshape([-1 if axis == position else 1 for axis in range(len(dims))])
    return gain


def normal_values(rng, extent, width, most, pieces=(), kind=jnp.bfloat16):
    gain = levels(rng, extent, pieces, -0.22, 0.18) if pieces else 1.0
    array = jax.random.normal(rng, extent, jnp.float32) * width * gain
    return jnp.minimum(jnp.maximum(array, -most), most).astype(kind)


def setup_inputs(seed: int = 0) -> dict:
    seeds = jax.random.split(jax.random.key(seed), 3)
    return {
        "right_side": draw_right_side(jax.random.fold_in(seeds[2], 71), 0),
        "guess": normal_values(seeds[1], (NR, NT), 1.0, 6.0, ((0, 8), (1, 4)), jnp.float32),
    }


def coefficients(row_float, spacing):
    radius = 1.0 + (row_float + 0.5) * spacing
    offset_ratio = 0.5 * spacing / radius
    outward = 1.0 + offset_ratio
    inward = 1.0 - offset_ratio
    angular = 1.0 / (radius * radius)
    centre = 2.0 + 2.0 * angular
    return outward, inward, angular, centre


def relax_cells(padded, source, stencil, chosen):
    outward, inward, angular, centre = stencil
    middle = padded[1:-1, 1:-1]
    updated = (source + outward * padded[2:, 1:-1] + inward * padded[:-2, 1:-1]
               + angular * (padded[1:-1, 2:] + padded[1:-1, :-2])) / centre
    return jnp.where(chosen, updated, middle)


def apply_operator(padded, stencil):
    outward, inward, angular, centre = stencil
    middle = padded[1:-1, 1:-1]
    return (centre * middle - outward * padded[2:, 1:-1] - inward * padded[:-2, 1:-1]
            - angular * (padded[1:-1, 2:] + padded[1:-1, :-2]))


def restrict_grid(padded):
    height = padded.shape[0] - 2
    breadth = padded.shape[1] - 2
    row_sum = (padded[0:height:2] + 3.0 * padded[1:height + 1:2] + 3.0 * padded[2:height + 2:2]
               + padded[3:height + 3:2]) * 0.125
    col_sum = (row_sum[:, 0:breadth:2] + 3.0 * row_sum[:, 1:breadth + 1:2] + 3.0 * row_sum[:, 2:breadth + 2:2]
               + row_sum[:, 3:breadth + 3:2]) * 0.125
    return 4.0 * col_sum


def prolong_grid(padded):
    centre_rep = jnp.repeat(padded[1:-1], 2, axis=0)
    below_rep = jnp.repeat(padded[:-2], 2, axis=0)
    above_rep = jnp.repeat(padded[2:], 2, axis=0)
    row_ids = jnp.arange(centre_rep.shape[0], dtype=jnp.int32)[:, None]
    stretched = 0.75 * centre_rep + 0.25 * jnp.where(row_ids % 2 == 0, below_rep, above_rep)
    mid_cols = jnp.repeat(stretched[:, 1:-1], 2, axis=1)
    left_cols = jnp.repeat(stretched[:, :-2], 2, axis=1)
    right_cols = jnp.repeat(stretched[:, 2:], 2, axis=1)
    col_ids = jnp.arange(mid_cols.shape[1], dtype=jnp.int32)[None, :]
    return 0.75 * mid_cols + 0.25 * jnp.where(col_ids % 2 == 0, left_cols, right_cols)


def wrap_pad(values, margin):
    values = jnp.pad(values, ((0, 0), (margin, margin)), mode="wrap")
    return jnp.pad(values, ((margin, margin), (0, 0)))


def cycle_local(level_at, iterate, source):
    height, breadth = source.shape
    spacing = 2.0 * math.pi / breadth
    row_ids = jnp.arange(height, dtype=jnp.int32)[:, None]
    col_ids = jnp.arange(breadth, dtype=jnp.int32)[None, :]
    stencil = coefficients(row_ids.astype(jnp.float32), spacing)
    red_cells = (row_ids + col_ids) % 2 == 0
    black_cells = jnp.logical_not(red_cells)

    def colour_sweep(values):
        values = relax_cells(wrap_pad(values, 1), source, stencil, red_cells)
        return relax_cells(wrap_pad(values, 1), source, stencil, black_cells)

    if level_at == LEVELS - 1:
        for _ in range(COARSE_SWEEPS):
            iterate = colour_sweep(iterate)
        return iterate
    for _ in range(PRE):
        iterate = colour_sweep(iterate)
    remainder = source - apply_operator(wrap_pad(iterate, 1), stencil)
    coarse_source = restrict_grid(wrap_pad(remainder, 1))
    correction = cycle_local(level_at + 1, jnp.zeros_like(coarse_source), coarse_source)
    iterate = iterate + prolong_grid(wrap_pad(correction, 1))
    for _ in range(POST):
        iterate = colour_sweep(iterate)
    return iterate


def reference(right_side, guess):
    solution = cycle_local(0, guess, right_side)
    height, breadth = right_side.shape
    row_ids = jnp.arange(height, dtype=jnp.int32)[:, None]
    stencil = coefficients(row_ids.astype(jnp.float32), 2.0 * math.pi / breadth)
    residual = right_side - apply_operator(wrap_pad(solution, 1), stencil)
    return solution, residual
```

```python
import math

import jax
import jax.numpy as jnp
from jax import lax
from jax.experimental import pallas as pl
from jax.experimental.pallas import tpu as pltpu
from jax.sharding import PartitionSpec as P

LEVELS = 8
PRE = 2
POST = 2
COARSE_SWEEPS = 8
SPREAD = 3
PAD = 8
UP = 8
LANES = 128
SIDE = 64
HIGH = lax.Precision.HIGHEST


def iota(shape, dim):
    return lax.broadcasted_iota(jnp.int32, shape, dim)


def dot(a, b):
    return lax.dot_general(
        a, b, (((1,), (0,)), ((), ())), precision=HIGH, preferred_element_type=jnp.float32
    )


def wide(x, breadth):
    return x if breadth == LANES else jnp.concatenate([x] * (breadth // LANES), axis=1)


def chunk_of(rows, breadth):
    units = rows // 8
    best = 1
    for n in range(1, units + 1):
        if units % n == 0 and n * 8 * breadth <= 20 * 1024:
            best = n
    return 8 * best


class Level:
    def __init__(self, v, g, cf, spacing, total, first):
        self.v, self.g, self.cf = v, g, cf
        self.rows, self.breadth = g.shape
        self.spacing, self.total, self.first = spacing, total, first
        self.n = chunk_of(self.rows, self.breadth)

    def fill(self):
        shape = (self.rows, LANES)
        ids = self.first + iota(shape, 0)
        radius = 1.0 + (ids.astype(jnp.float32) + 0.5) * self.spacing
        ratio = 0.5 * self.spacing / radius
        angular = 1.0 / (radius * radius)
        centre = 2.0 + 2.0 * angular
        inside = jnp.logical_and(ids >= 0, ids < self.total)
        self.cf[pl.ds(0 * self.rows, self.rows), :] = 1.0 + ratio
        self.cf[pl.ds(1 * self.rows, self.rows), :] = 1.0 - ratio
        self.cf[pl.ds(2 * self.rows, self.rows), :] = angular
        self.cf[pl.ds(3 * self.rows, self.rows), :] = centre
        self.cf[pl.ds(4 * self.rows, self.rows), :] = jnp.where(inside, 1.0 / centre, 0.0)
        zero = jnp.zeros((PAD, self.breadth), jnp.float32)
        self.v[pl.ds(0, PAD), :] = zero
        self.v[pl.ds(PAD + self.rows, PAD), :] = zero

    def loop(self, body):
        steps = self.rows // self.n
        if steps == 1:
            body(0)
        else:
            def step(k, carry):
                body(pl.multiple_of(k * self.n, 8))
                return carry

            lax.fori_loop(0, steps, step, 0)

    def coef(self, which, b):
        return wide(self.cf[pl.ds(which * self.rows + b, self.n), :], self.breadth)

    def parity(self):
        shape = (self.n, LANES)
        return wide(((iota(shape, 0) + iota(shape, 1)) & 1).astype(jnp.float32), self.breadth)

    def neighbours(self, b):
        near = self.v[pl.ds(b, self.n + 2 * PAD), :]
        mid = near[PAD : PAD + self.n]
        below = near[PAD - 1 : PAD - 1 + self.n]
        above = near[PAD + 1 : PAD + 1 + self.n]
        sides = pltpu.roll(mid, 1, 1) + pltpu.roll(mid, self.breadth - 1, 1)
        total = (
            self.coef(0, b) * above + self.coef(1, b) * below + self.coef(2, b) * sides
        )
        return mid, total

    def half(self, colour):
        chosen = self.parity() == float(colour)

        def body(b):
            mid, total = self.neighbours(b)
            updated = (self.g[pl.ds(b, self.n), :] + total) * self.coef(4, b)
            self.v[pl.ds(b + PAD, self.n), :] = jnp.where(chosen, updated, mid)

        self.loop(body)

    def sweeps(self, count):
        for _ in range(count):
            self.half(0)
            self.half(1)

    def sweeps_from_zero(self, count):
        red = self.parity() == 0.0

        def body(b):
            updated = self.g[pl.ds(b, self.n), :] * self.coef(4, b)
            self.v[pl.ds(b + PAD, self.n), :] = jnp.where(red, updated, 0.0)

        self.loop(body)
        self.half(1)
        self.sweeps(count - 1)

    def residual(self, out):
        def body(b):
            mid, total = self.neighbours(b)
            s = self.g[pl.ds(b, self.n), :] - (self.coef(3, b) * mid - total)
            out[pl.ds(b, self.n), :] = jnp.where(self.coef(4, b) != 0.0, s, 0.0)

        self.loop(body)

    def add(self, p):
        inside = wide(self.cf[pl.ds(4 * self.rows, self.rows), :], self.breadth) != 0.0
        at = pl.ds(PAD, self.rows)
        self.v[at, :] = self.v[at, :] + jnp.where(inside, p, 0.0)


def one(cond):
    return jnp.where(cond, 1.0, 0.0).astype(jnp.float32)


def restricted(s, halo, period):
    rows, breadth = s.shape
    shape = (rows // 2, rows)
    gap = iota(shape, 1) - 2 * iota(shape, 0)
    weights = jnp.where(
        jnp.logical_or(gap == 0, gap == 1),
        0.375,
        jnp.where(jnp.logical_or(gap == -1, gap == 2), 0.125, 0.0),
    ).astype(jnp.float32)
    t = dot(weights, s[...])
    u = 0.5 * (
        pltpu.roll(t, 1, 1)
        + 3.0 * t
        + 3.0 * pltpu.roll(t, breadth - 1, 1)
        + pltpu.roll(t, breadth - 2, 1)
    )
    own = breadth - (LANES if halo else 0)
    tiles = []
    if own >= 2 * LANES:
        shape = (2 * LANES, LANES)
        pick = one(iota(shape, 0) == 2 * iota(shape, 1))
        for k in range(own // (2 * LANES)):
            tiles.append(dot(u[:, 2 * LANES * k : 2 * LANES * (k + 1)], pick))
    else:
        shape = (LANES, LANES)
        pick = one(iota(shape, 0) == 2 * (iota(shape, 1) % (period // 2)))
        tiles.append(dot(u, pick))
    if halo:
        shape = (LANES, LANES)
        j, i = iota(shape, 0), iota(shape, 1)
        right = jnp.logical_and(j == 2 * i, j < SIDE)
        left = jnp.logical_and(j == 2 * i - LANES, j >= SIDE)
        tiles.append(dot(u[:, own:], one(jnp.logical_or(right, left))))
    return tiles[0] if len(tiles) == 1 else jnp.concatenate(tiles, axis=1)


def prolonged(e, rows, shift, halo, fine_period):
    breadth = e.shape[1]
    a = 0.75 * e + 0.25 * pltpu.roll(e, 1, 1)
    b = 0.75 * e + 0.25 * pltpu.roll(e, breadth - 1, 1)
    own = breadth - (LANES if halo else 0)
    tiles = []

    def pair(k):
        at = slice(LANES * k, LANES * (k + 1))
        return jnp.concatenate([a[:, at], b[:, at]], axis=1)

    if fine_period > LANES:
        shape = (2 * LANES, 2 * LANES)
        i, j = iota(shape, 0), iota(shape, 1)
        spread = one(j == jnp.where(i < LANES, 2 * i, 2 * (i - LANES) + 1))
        for k in range(own // LANES):
            tiles.append(dot(pair(k), spread))
    else:
        shape = (2 * LANES, LANES)
        i, j = iota(shape, 0), iota(shape, 1) % fine_period
        spread = one(j == jnp.where(i < LANES, 2 * i, 2 * (i - LANES) + 1))
        tiles.append(dot(pair(0), spread))
    if halo:
        shape = (2 * LANES, LANES)
        i, j = iota(shape, 0), iota(shape, 1)
        lane = i % LANES
        source = jnp.where(j < SIDE, j // 2, j // 2 + SIDE)
        spread = one(jnp.logical_and(lane == source, i // LANES == j % 2))
        tiles.append(dot(pair(own // LANES), spread))
    p = tiles[0] if len(tiles) == 1 else jnp.concatenate(tiles, axis=1)
    shape = (rows, e.shape[0])
    i, c = iota(shape, 0), iota(shape, 1)
    near = i // 2 + shift
    far = near + jnp.where(i % 2 == 0, -1, 1)
    weights = jnp.where(c == near, 0.75, jnp.where(c == far, 0.25, 0.0)).astype(jnp.float32)
    return dot(weights, p)


def down_kernel(height, total, spacings, place, v, hv, g, hg, top, bottom, *refs):
    outs, scratch = refs[: 2 * SPREAD + 1], refs[2 * SPREAD + 1 :]
    halo = UP << SPREAD
    breadth = v.shape[1]
    rows = height + 2 * halo
    vb, gb = scratch[0], scratch[1]
    at = pl.ds(PAD + halo, height)
    vb[at, pl.ds(0, breadth)] = v[...]
    vb[at, pl.ds(breadth, LANES)] = hv[...]
    vb[pl.ds(PAD, halo), :] = top[pl.ds(0, halo), :]
    vb[pl.ds(PAD + halo + height, halo), :] = bottom[pl.ds(0, halo), :]
    at = pl.ds(halo, height)
    gb[at, pl.ds(0, breadth)] = g[...]
    gb[at, pl.ds(breadth, LANES)] = hg[...]
    gb[pl.ds(0, halo), :] = top[pl.ds(halo, halo), :]
    gb[pl.ds(halo + height, halo), :] = bottom[pl.ds(halo, halo), :]
    for l in range(SPREAD):
        vb, gb, cf, s = scratch[4 * l : 4 * l + 4]
        edge = halo >> l
        own = height >> l
        level = Level(vb, gb, cf, spacings[l], total >> l, place[0] * own - edge)
        level.fill()
        if l == 0:
            level.sweeps(PRE)
        else:
            level.sweeps_from_zero(PRE)
        outs[2 * l][...] = vb[pl.ds(PAD + edge - UP, own + 2 * UP), :]
        outs[2 * l + 1][...] = gb[pl.ds(edge - UP, own + 2 * UP), :]
        level.residual(s)
        coarse = restricted(s, True, None)
        if l + 1 < SPREAD:
            scratch[4 * (l + 1) + 1][...] = coarse
        else:
            edge, own = edge // 2, own // 2
            outs[2 * SPREAD][...] = coarse[edge : edge + own, : outs[2 * SPREAD].shape[1]]


def up_kernel(height, total, spacings, sizes, place, gathered, *refs):
    ins, refs = refs[: 2 * SPREAD], refs[2 * SPREAD :]
    out_v, out_s, scratch = refs[0], refs[1], refs[2:]
    rads, angs = sizes
    whole = []
    for l in range(SPREAD, LEVELS):
        v, g, cf, s = scratch[4 * (l - SPREAD) : 4 * (l - SPREAD) + 4]
        whole.append((Level(v, g, cf, spacings[l], total >> l, 0), s))
    g = whole[0][0].g
    piece = gathered.shape[1:]
    for r in range(rads):
        for a in range(angs):
            g[pl.ds(r * piece[0], piece[0]), pl.ds(a * piece[1], piece[1])] = gathered[r * angs + a]

    def period(l):
        return (piece[1] * angs) >> (l - SPREAD)

    for l in range(SPREAD, LEVELS):
        level, s = whole[l - SPREAD]
        level.fill()
        if l == LEVELS - 1:
            level.sweeps_from_zero(COARSE_SWEEPS)
        else:
            level.sweeps_from_zero(PRE)
            level.residual(s)
            whole[l + 1 - SPREAD][0].g[...] = restricted(s, False, period(l))
    for l in range(LEVELS - 2, SPREAD - 1, -1):
        level, s = whole[l - SPREAD]
        coarse = whole[l + 1 - SPREAD][0]
        e = coarse.v[pl.ds(PAD, coarse.rows), :]
        level.add(prolonged(e, level.rows, 0, False, period(l)))
        level.sweeps(POST)
    v = whole[0][0].v
    start = place[1] * piece[1]
    across = piece[1] * angs
    at = pl.ds(pl.multiple_of(place[0] * piece[0], 8), piece[0] + 2 * UP)
    after = pl.multiple_of(lax.rem(start + piece[1], across), LANES)
    before = pl.multiple_of(lax.rem(start + across - LANES, across), LANES)
    tile = (piece[0] + 2 * UP, LANES)
    halo = jnp.where(iota(tile, 1) < SIDE, v[at, pl.ds(after, LANES)], v[at, pl.ds(before, LANES)])
    own = v[at, pl.ds(pl.multiple_of(start, LANES), piece[1])]
    e = jnp.concatenate([own, halo], axis=1)
    base = 4 * (LEVELS - SPREAD)
    for l in range(SPREAD - 1, -1, -1):
        v, cf = scratch[base + 2 * l : base + 2 * l + 2]
        own = height >> l
        level = Level(v, ins[2 * l + 1], cf, spacings[l], total >> l, place[0] * own - UP)
        level.fill()
        v[pl.ds(PAD, level.rows), :] = ins[2 * l][...]
        level.add(prolonged(e, level.rows, UP // 2, True, 2 * LANES))
        level.sweeps(POST)
        e = v[pl.ds(PAD, level.rows), :]
    s = scratch[-1]
    level.residual(s)
    breadth = out_v.shape[1]
    out_v[...] = v[pl.ds(PAD + UP, height), pl.ds(0, breadth)]
    out_s[...] = s[pl.ds(UP, height), pl.ds(0, breadth)]


def f32(*shape):
    return jax.ShapeDtypeStruct(shape, jnp.float32)


def vmem(*shape):
    return pltpu.VMEM(shape, jnp.float32)


def local(right_side, guess):
    height, breadth = right_side.shape
    rads, angs = lax.axis_size("rad"), lax.axis_size("ang")
    total = height * rads
    spacings = [2.0 * math.pi / ((breadth * angs) >> l) for l in range(LEVELS)]
    halo = UP << SPREAD
    up = [(i, (i + 1) % angs) for i in range(angs)]
    down = [(j, i) for i, j in up]
    first = jnp.concatenate([guess[:, :SIDE], right_side[:, :SIDE]], axis=1)
    last = jnp.concatenate([guess[:, -SIDE:], right_side[:, -SIDE:]], axis=1)
    after = lax.ppermute(first, "ang", down)
    before = lax.ppermute(last, "ang", up)
    halo_v = jnp.concatenate([after[:, :SIDE], before[:, :SIDE]], axis=1)
    halo_g = jnp.concatenate([after[:, SIDE:], before[:, SIDE:]], axis=1)

    def edge(at):
        top = jnp.concatenate([guess[at], halo_v[at]], axis=1)
        low = jnp.concatenate([right_side[at], halo_g[at]], axis=1)
        return jnp.concatenate([top, low], axis=0)

    up = [(i, i + 1) for i in range(rads - 1)]
    down = [(j, i) for i, j in up]
    above = lax.ppermute(edge(slice(-halo, None)), "rad", up)
    below = lax.ppermute(edge(slice(0, halo)), "rad", down)
    place = jnp.stack([lax.axis_index("rad"), lax.axis_index("ang")]).astype(jnp.int32)
    smem = pl.BlockSpec(memory_space=pltpu.SMEM)
    full = pl.BlockSpec(memory_space=pltpu.VMEM)

    kept, scratch = [], []
    for l in range(SPREAD):
        rows, cols = height >> l, (breadth >> l) + LANES
        kept += [f32(rows + 2 * UP, cols)] * 2
        rows += 2 * (halo >> l)
        scratch += [vmem(rows + 2 * PAD, cols), vmem(rows, cols), vmem(5 * rows, LANES), vmem(rows, cols)]
    piece = (height >> SPREAD, breadth >> SPREAD)
    *kept, coarse = pl.pallas_call(
        lambda *refs: down_kernel(height, total, spacings, *refs),
        out_shape=kept + [f32(*piece)],
        in_specs=[smem] + [full] * 6,
        out_specs=[full] * (2 * SPREAD + 1),
        scratch_shapes=scratch,
        compiler_params=pltpu.CompilerParams(vmem_limit_bytes=50 * 1024 * 1024),
        name="down",
    )(place, guess, halo_v, right_side, halo_g, above, below)

    gathered = lax.all_gather(coarse, ("rad", "ang"), axis=0, tiled=False)
    scratch = []
    for l in range(SPREAD, LEVELS):
        rows, cols = total >> l, max(LANES, (breadth * angs) >> l)
        scratch += [vmem(rows + 2 * PAD, cols), vmem(rows, cols), vmem(5 * rows, LANES), vmem(rows, cols)]
    for l in range(SPREAD):
        rows, cols = (height >> l) + 2 * UP, (breadth >> l) + LANES
        scratch += [vmem(rows + 2 * PAD, cols), vmem(5 * rows, LANES)]
    scratch.append(vmem(height + 2 * UP, breadth + LANES))
    return tuple(
        pl.pallas_call(
            lambda *refs: up_kernel(height, total, spacings, (rads, angs), *refs),
            out_shape=[f32(height, breadth)] * 2,
            in_specs=[smem] + [full] * (2 * SPREAD + 1),
            out_specs=[full] * 2,
            scratch_shapes=scratch,
            compiler_params=pltpu.CompilerParams(vmem_limit_bytes=50 * 1024 * 1024),
            name="up",
        )(place, gathered, *kept)
    )


def solution(mesh):
    placed = (P("rad", "ang"), P("rad", "ang"))
    return jax.shard_map(
        local,
        mesh=mesh,
        in_specs=placed,
        out_specs=(P("rad", "ang"), P("rad", "ang")),
        check_vma=False,
    )
```

```python
import math

import jax
import jax.numpy as jnp
from jax import lax
from jax.experimental import pallas as pl
from jax.experimental.pallas import tpu as pltpu
from jax.sharding import PartitionSpec as P

LEVELS = 8
PRE = 2
POST = 2
COARSE_SWEEPS = 8
SPREAD = 3
PAD = 8
UP = 8
LANES = 128
SIDE = 64
HIGH = lax.Precision.HIGHEST


def iota(shape, dim):
    return lax.broadcasted_iota(jnp.int32, shape, dim)


def dot(a, b):
    return lax.dot_general(
        a, b, (((1,), (0,)), ((), ())), precision=HIGH, preferred_element_type=jnp.float32
    )


def wide(x, breadth):
    return x if breadth == LANES else jnp.concatenate([x] * (breadth // LANES), axis=1)


def chunk_of(rows, breadth):
    units = rows // 8
    best = 1
    for n in range(1, units + 1):
        if units % n == 0 and n * 8 * breadth <= 20 * 1024:
            best = n
    return 8 * best


class Level:
    def __init__(self, v, g, cf, spacing, total, first):
        self.v, self.g, self.cf = v, g, cf
        self.rows, self.breadth = g.shape
        self.spacing, self.total, self.first = spacing, total, first
        self.n = chunk_of(self.rows, self.breadth)

    def fill(self):
        shape = (self.rows, LANES)
        ids = self.first + iota(shape, 0)
        radius = 1.0 + (ids.astype(jnp.float32) + 0.5) * self.spacing
        ratio = 0.5 * self.spacing / radius
        angular = 1.0 / (radius * radius)
        centre = 2.0 + 2.0 * angular
        inside = jnp.logical_and(ids >= 0, ids < self.total)
        self.cf[pl.ds(0 * self.rows, self.rows), :] = 1.0 + ratio
        self.cf[pl.ds(1 * self.rows, self.rows), :] = 1.0 - ratio
        self.cf[pl.ds(2 * self.rows, self.rows), :] = angular
        self.cf[pl.ds(3 * self.rows, self.rows), :] = centre
        self.cf[pl.ds(4 * self.rows, self.rows), :] = jnp.where(inside, 1.0 / centre, 0.0)
        zero = jnp.zeros((PAD, self.breadth), jnp.float32)
        self.v[pl.ds(0, PAD), :] = zero
        self.v[pl.ds(PAD + self.rows, PAD), :] = zero

    def loop(self, body):
        steps = self.rows // self.n
        if steps == 1:
            body(0)
        else:
            def step(k, carry):
                body(pl.multiple_of(k * self.n, 8))
                return carry

            lax.fori_loop(0, steps, step, 0)

    def coef(self, which, b):
        return wide(self.cf[pl.ds(which * self.rows + b, self.n), :], self.breadth)

    def parity(self):
        shape = (self.n, LANES)
        return wide(((iota(shape, 0) + iota(shape, 1)) & 1).astype(jnp.float32), self.breadth)

    def neighbours(self, b):
        near = self.v[pl.ds(b, self.n + 2 * PAD), :]
        mid = near[PAD : PAD + self.n]
        below = near[PAD - 1 : PAD - 1 + self.n]
        above = near[PAD + 1 : PAD + 1 + self.n]
        sides = pltpu.roll(mid, 1, 1) + pltpu.roll(mid, self.breadth - 1, 1)
        total = (
            self.coef(0, b) * above + self.coef(1, b) * below + self.coef(2, b) * sides
        )
        return mid, total

    def half(self, colour):
        chosen = self.parity() == float(colour)

        def body(b):
            mid, total = self.neighbours(b)
            updated = (self.g[pl.ds(b, self.n), :] + total) * self.coef(4, b)
            self.v[pl.ds(b + PAD, self.n), :] = jnp.where(chosen, updated, mid)

        self.loop(body)

    def sweeps(self, count):
        for _ in range(count):
            self.half(0)
            self.half(1)

    def sweeps_from_zero(self, count):
        red = self.parity() == 0.0

        def body(b):
            updated = self.g[pl.ds(b, self.n), :] * self.coef(4, b)
            self.v[pl.ds(b + PAD, self.n), :] = jnp.where(red, updated, 0.0)

        self.loop(body)
        self.half(1)
        self.sweeps(count - 1)

    def residual(self, out):
        def body(b):
            mid, total = self.neighbours(b)
            s = self.g[pl.ds(b, self.n), :] - (self.coef(3, b) * mid - total)
            out[pl.ds(b, self.n), :] = jnp.where(self.coef(4, b) != 0.0, s, 0.0)

        self.loop(body)

    def add(self, p):
        inside = wide(self.cf[pl.ds(4 * self.rows, self.rows), :], self.breadth) != 0.0
        at = pl.ds(PAD, self.rows)
        self.v[at, :] = self.v[at, :] + jnp.where(inside, p, 0.0)


def one(cond):
    return jnp.where(cond, 1.0, 0.0).astype(jnp.float32)


def restricted(s, halo, period):
    rows, breadth = s.shape
    shape = (rows // 2, rows)
    gap = iota(shape, 1) - 2 * iota(shape, 0)
    weights = jnp.where(
        jnp.logical_or(gap == 0, gap == 1),
        0.375,
        jnp.where(jnp.logical_or(gap == -1, gap == 2), 0.125, 0.0),
    ).astype(jnp.float32)
    t = dot(weights, s[...])
    u = 0.5 * (
        pltpu.roll(t, 1, 1)
        + 3.0 * t
        + 3.0 * pltpu.roll(t, breadth - 1, 1)
        + pltpu.roll(t, breadth - 2, 1)
    )
    own = breadth - (LANES if halo else 0)
    tiles = []
    if own >= 2 * LANES:
        shape = (2 * LANES, LANES)
        pick = one(iota(shape, 0) == 2 * iota(shape, 1))
        for k in range(own // (2 * LANES)):
            tiles.append(dot(u[:, 2 * LANES * k : 2 * LANES * (k + 1)], pick))
    else:
        shape = (LANES, LANES)
        pick = one(iota(shape, 0) == 2 * (iota(shape, 1) % (period // 2)))
        tiles.append(dot(u, pick))
    if halo:
        shape = (LANES, LANES)
        j, i = iota(shape, 0), iota(shape, 1)
        right = jnp.logical_and(j == 2 * i, j < SIDE)
        left = jnp.logical_and(j == 2 * i - LANES, j >= SIDE)
        tiles.append(dot(u[:, own:], one(jnp.logical_or(right, left))))
    return tiles[0] if len(tiles) == 1 else jnp.concatenate(tiles, axis=1)


def prolonged(e, rows, shift, halo, fine_period):
    breadth = e.shape[1]
    a = 0.75 * e + 0.25 * pltpu.roll(e, 1, 1)
    b = 0.75 * e + 0.25 * pltpu.roll(e, breadth - 1, 1)
    own = breadth - (LANES if halo else 0)
    tiles = []

    def pair(k):
        at = slice(LANES * k, LANES * (k + 1))
        return jnp.concatenate([a[:, at], b[:, at]], axis=1)

    if fine_period > LANES:
        shape = (2 * LANES, 2 * LANES)
        i, j = iota(shape, 0), iota(shape, 1)
        spread = one(j == jnp.where(i < LANES, 2 * i, 2 * (i - LANES) + 1))
        for k in range(own // LANES):
            tiles.append(dot(pair(k), spread))
    else:
        shape = (2 * LANES, LANES)
        i, j = iota(shape, 0), iota(shape, 1) % fine_period
        spread = one(j == jnp.where(i < LANES, 2 * i, 2 * (i - LANES) + 1))
        tiles.append(dot(pair(0), spread))
    if halo:
        shape = (2 * LANES, LANES)
        i, j = iota(shape, 0), iota(shape, 1)
        lane = i % LANES
        source = jnp.where(j < SIDE, j // 2, j // 2 + SIDE)
        spread = one(jnp.logical_and(lane == source, i // LANES == j % 2))
        tiles.append(dot(pair(own // LANES), spread))
    p = tiles[0] if len(tiles) == 1 else jnp.concatenate(tiles, axis=1)
    shape = (rows, e.shape[0])
    i, c = iota(shape, 0), iota(shape, 1)
    near = i // 2 + shift
    far = near + jnp.where(i % 2 == 0, -1, 1)
    weights = jnp.where(c == near, 0.75, jnp.where(c == far, 0.25, 0.0)).astype(jnp.float32)
    return dot(weights, p)


def down_kernel(height, total, spacings, place, v, hv, g, hg, top, bottom, htop, hbottom, *refs):
    outs, scratch = refs[: 2 * SPREAD + 1], refs[2 * SPREAD + 1 :]
    halo = UP << SPREAD
    breadth = v.shape[1]
    rows = height + 2 * halo
    vb, gb = scratch[0], scratch[1]
    at = pl.ds(PAD + halo, height)
    vb[at, pl.ds(0, breadth)] = v[...]
    vb[at, pl.ds(breadth, LANES)] = hv[...]
    for buf, take, shift in ((vb, 0, PAD), (gb, halo, 0)):
        for at, block, corner in ((0, top, htop), (halo + height, bottom, hbottom)):
            at = pl.ds(at + shift, halo)
            buf[at, pl.ds(0, breadth)] = block[pl.ds(take, halo), :]
            buf[at, pl.ds(breadth, LANES)] = corner[pl.ds(take, halo), :]
    at = pl.ds(halo, height)
    gb[at, pl.ds(0, breadth)] = g[...]
    gb[at, pl.ds(breadth, LANES)] = hg[...]
    for l in range(SPREAD):
        vb, gb, cf, s = scratch[4 * l : 4 * l + 4]
        edge = halo >> l
        own = height >> l
        level = Level(vb, gb, cf, spacings[l], total >> l, place[0] * own - edge)
        level.fill()
        if l == 0:
            level.sweeps(PRE)
        else:
            level.sweeps_from_zero(PRE)
        outs[2 * l][...] = vb[pl.ds(PAD + edge - UP, own + 2 * UP), :]
        outs[2 * l + 1][...] = gb[pl.ds(edge - UP, own + 2 * UP), :]
        level.residual(s)
        coarse = restricted(s, True, None)
        if l + 1 < SPREAD:
            scratch[4 * (l + 1) + 1][...] = coarse
        else:
            edge, own = edge // 2, own // 2
            outs[2 * SPREAD][...] = coarse[edge : edge + own, : outs[2 * SPREAD].shape[1]]


def up_kernel(height, total, spacings, sizes, place, gathered, *refs):
    ins, refs = refs[: 2 * SPREAD], refs[2 * SPREAD :]
    out_v, out_s, scratch = refs[0], refs[1], refs[2:]
    rads, angs = sizes
    whole = []
    for l in range(SPREAD, LEVELS):
        v, g, cf, s = scratch[4 * (l - SPREAD) : 4 * (l - SPREAD) + 4]
        whole.append((Level(v, g, cf, spacings[l], total >> l, 0), s))
    g = whole[0][0].g
    piece = gathered.shape[1:]
    for k, (r, a) in enumerate(gather_order(rads, angs)[1]):
        row = pl.multiple_of((place[0] ^ r) * piece[0], 8)
        col = pl.multiple_of((place[1] ^ a) * piece[1], LANES)
        g[pl.ds(row, piece[0]), pl.ds(col, piece[1])] = gathered[k]

    def period(l):
        return (piece[1] * angs) >> (l - SPREAD)

    for l in range(SPREAD, LEVELS):
        level, s = whole[l - SPREAD]
        level.fill()
        if l == LEVELS - 1:
            level.sweeps_from_zero(COARSE_SWEEPS)
        else:
            level.sweeps_from_zero(PRE)
            level.residual(s)
            whole[l + 1 - SPREAD][0].g[...] = restricted(s, False, period(l))
    for l in range(LEVELS - 2, SPREAD - 1, -1):
        level, s = whole[l - SPREAD]
        coarse = whole[l + 1 - SPREAD][0]
        e = coarse.v[pl.ds(PAD, coarse.rows), :]
        level.add(prolonged(e, level.rows, 0, False, period(l)))
        level.sweeps(POST)
    v = whole[0][0].v
    start = place[1] * piece[1]
    across = piece[1] * angs
    at = pl.ds(pl.multiple_of(place[0] * piece[0], 8), piece[0] + 2 * UP)
    after = pl.multiple_of(lax.rem(start + piece[1], across), LANES)
    before = pl.multiple_of(lax.rem(start + across - LANES, across), LANES)
    tile = (piece[0] + 2 * UP, LANES)
    halo = jnp.where(iota(tile, 1) < SIDE, v[at, pl.ds(after, LANES)], v[at, pl.ds(before, LANES)])
    own = v[at, pl.ds(pl.multiple_of(start, LANES), piece[1])]
    e = jnp.concatenate([own, halo], axis=1)
    base = 4 * (LEVELS - SPREAD)
    for l in range(SPREAD - 1, -1, -1):
        v, cf = scratch[base + 2 * l : base + 2 * l + 2]
        own = height >> l
        level = Level(v, ins[2 * l + 1], cf, spacings[l], total >> l, place[0] * own - UP)
        level.fill()
        v[pl.ds(PAD, level.rows), :] = ins[2 * l][...]
        level.add(prolonged(e, level.rows, UP // 2, True, 2 * LANES))
        level.sweeps(POST)
        e = v[pl.ds(PAD, level.rows), :]
    s = scratch[-1]
    level.residual(s)
    breadth = out_v.shape[1]
    out_v[...] = v[pl.ds(PAD + UP, height), pl.ds(0, breadth)]
    out_s[...] = s[pl.ds(UP, height), pl.ds(0, breadth)]


def gather_order(rads, angs):
    rounds = [("rad", 1 << k) for k in range(rads.bit_length() - 2, 0, -1)]
    rounds += [("ang", 1 << k) for k in range(angs.bit_length() - 1)]
    rounds += [("rad", 1)] if rads > 1 else []
    held = [(0, 0)]
    for axis, bit in rounds:
        held += [(r ^ bit, a) if axis == "rad" else (r, a ^ bit) for r, a in held]
    return rounds, held


def gather_pieces(piece, rads, angs):
    held = piece[None]
    for axis, bit in gather_order(rads, angs)[0]:
        pairs = [(i, i ^ bit) for i in range(lax.axis_size(axis))]
        held = jnp.concatenate([held, lax.ppermute(held, axis, pairs)], axis=0)
    return held


def f32(*shape):
    return jax.ShapeDtypeStruct(shape, jnp.float32)


def vmem(*shape):
    return pltpu.VMEM(shape, jnp.float32)


def local(right_side, guess):
    height, breadth = right_side.shape
    rads, angs = lax.axis_size("rad"), lax.axis_size("ang")
    total = height * rads
    spacings = [2.0 * math.pi / ((breadth * angs) >> l) for l in range(LEVELS)]
    halo = UP << SPREAD
    ring_up = [(i, (i + 1) % angs) for i in range(angs)]
    ring_down = [(j, i) for i, j in ring_up]
    up = [(i, i + 1) for i in range(rads - 1)]
    down = [(j, i) for i, j in up]

    def spread(x, y):
        last = jnp.concatenate([x[-halo:], y[-halo:]], axis=0)
        leading = jnp.concatenate([x[:halo], y[:halo]], axis=0)
        return lax.ppermute(last, "rad", up), lax.ppermute(leading, "rad", down)

    above, below = spread(guess, right_side)
    first = jnp.concatenate([guess[:, :SIDE], right_side[:, :SIDE]], axis=1)
    last = jnp.concatenate([guess[:, -SIDE:], right_side[:, -SIDE:]], axis=1)
    after = lax.ppermute(first, "ang", ring_down)
    before = lax.ppermute(last, "ang", ring_up)
    halo_v = jnp.concatenate([after[:, :SIDE], before[:, :SIDE]], axis=1)
    halo_g = jnp.concatenate([after[:, SIDE:], before[:, SIDE:]], axis=1)
    corner_above, corner_below = spread(halo_v, halo_g)
    place = jnp.stack([lax.axis_index("rad"), lax.axis_index("ang")]).astype(jnp.int32)
    smem = pl.BlockSpec(memory_space=pltpu.SMEM)
    full = pl.BlockSpec(memory_space=pltpu.VMEM)

    kept, scratch = [], []
    for l in range(SPREAD):
        rows, cols = height >> l, (breadth >> l) + LANES
        kept += [f32(rows + 2 * UP, cols)] * 2
        rows += 2 * (halo >> l)
        scratch += [vmem(rows + 2 * PAD, cols), vmem(rows, cols), vmem(5 * rows, LANES), vmem(rows, cols)]
    piece = (height >> SPREAD, breadth >> SPREAD)
    *kept, coarse = pl.pallas_call(
        lambda *refs: down_kernel(height, total, spacings, *refs),
        out_shape=kept + [f32(*piece)],
        in_specs=[smem] + [full] * 8,
        out_specs=[full] * (2 * SPREAD + 1),
        scratch_shapes=scratch,
        compiler_params=pltpu.CompilerParams(vmem_limit_bytes=50 * 1024 * 1024),
        name="down",
    )(place, guess, halo_v, right_side, halo_g, above, below, corner_above, corner_below)

    gathered = gather_pieces(coarse, rads, angs)
    scratch = []
    for l in range(SPREAD, LEVELS):
        rows, cols = total >> l, max(LANES, (breadth * angs) >> l)
        scratch += [vmem(rows + 2 * PAD, cols), vmem(rows, cols), vmem(5 * rows, LANES), vmem(rows, cols)]
    for l in range(SPREAD):
        rows, cols = (height >> l) + 2 * UP, (breadth >> l) + LANES
        scratch += [vmem(rows + 2 * PAD, cols), vmem(5 * rows, LANES)]
    scratch.append(vmem(height + 2 * UP, breadth + LANES))
    return tuple(
        pl.pallas_call(
            lambda *refs: up_kernel(height, total, spacings, (rads, angs), *refs),
            out_shape=[f32(height, breadth)] * 2,
            in_specs=[smem] + [full] * (2 * SPREAD + 1),
            out_specs=[full] * 2,
            scratch_shapes=scratch,
            compiler_params=pltpu.CompilerParams(vmem_limit_bytes=50 * 1024 * 1024),
            name="up",
        )(place, gathered, *kept)
    )


def solution(mesh):
    placed = (P("rad", "ang"), P("rad", "ang"))
    return jax.shard_map(
        local,
        mesh=mesh,
        in_specs=placed,
        out_specs=(P("rad", "ang"), P("rad", "ang")),
        check_vma=False,
    )
```

```python
import math

import jax
import jax.numpy as jnp
from jax import lax
from jax.experimental import pallas as pl
from jax.experimental.pallas import tpu as pltpu
from jax.sharding import PartitionSpec as P

LEVELS = 8
PRE = 2
POST = 2
COARSE_SWEEPS = 8
SPREAD = 3
PAD = 8
UP = 8
LANES = 128
SIDE = 64


def iota(shape, dim):
    return lax.broadcasted_iota(jnp.int32, shape, dim)


def thirds(x):
    high = x.astype(jnp.bfloat16)
    rest = x - high.astype(jnp.float32)
    middle = rest.astype(jnp.bfloat16)
    return high, middle, (rest - middle.astype(jnp.float32)).astype(jnp.bfloat16)


def product(a, b):
    return lax.dot_general(a, b, (((1,), (0,)), ((), ())), preferred_element_type=jnp.float32)


def dot(a, b, exact):
    if exact == 0:
        a = a.astype(jnp.bfloat16)
        high, middle, low = [product(a, x) for x in thirds(b)]
    else:
        b = b.astype(jnp.bfloat16)
        high, middle, low = [product(x, b) for x in thirds(a)]
    return high + (middle + low)


def wide(x, breadth):
    return x if breadth == LANES else jnp.concatenate([x] * (breadth // LANES), axis=1)


def chunk_of(rows, breadth):
    units = rows // 8
    best = 1
    for n in range(1, units + 1):
        if units % n == 0 and n * 8 * breadth <= 80 * 1024:
            best = n
    return 8 * best


class Level:
    def __init__(self, v, g, cf, spacing, total, first):
        self.v, self.g, self.cf = v, g, cf
        self.rows, self.breadth = g.shape
        self.spacing, self.total, self.first = spacing, total, first
        self.n = chunk_of(self.rows, self.breadth)

    def fill(self):
        shape = (self.rows, LANES)
        ids = self.first + iota(shape, 0)
        radius = 1.0 + (ids.astype(jnp.float32) + 0.5) * self.spacing
        ratio = 0.5 * self.spacing / radius
        angular = 1.0 / (radius * radius)
        centre = 2.0 + 2.0 * angular
        inside = jnp.logical_and(ids >= 0, ids < self.total)
        self.cf[pl.ds(0 * self.rows, self.rows), :] = 1.0 + ratio
        self.cf[pl.ds(1 * self.rows, self.rows), :] = 1.0 - ratio
        self.cf[pl.ds(2 * self.rows, self.rows), :] = angular
        self.cf[pl.ds(3 * self.rows, self.rows), :] = centre
        self.cf[pl.ds(4 * self.rows, self.rows), :] = jnp.where(inside, 1.0 / centre, 0.0)
        zero = jnp.zeros((PAD, self.breadth), jnp.float32)
        self.v[pl.ds(0, PAD), :] = zero
        self.v[pl.ds(PAD + self.rows, PAD), :] = zero

    def loop(self, body):
        steps = self.rows // self.n
        if steps == 1:
            body(0)
        else:
            def step(k, carry):
                body(pl.multiple_of(k * self.n, 8))
                return carry

            lax.fori_loop(0, steps, step, 0)

    def coef(self, which, b):
        return wide(self.cf[pl.ds(which * self.rows + b, self.n), :], self.breadth)

    def parity(self):
        shape = (self.n, LANES)
        return wide(((iota(shape, 0) + iota(shape, 1)) & 1).astype(jnp.float32), self.breadth)

    def neighbours(self, b):
        near = self.v[pl.ds(b, self.n + 2 * PAD), :]
        mid = near[PAD : PAD + self.n]
        below = near[PAD - 1 : PAD - 1 + self.n]
        above = near[PAD + 1 : PAD + 1 + self.n]
        sides = pltpu.roll(mid, 1, 1) + pltpu.roll(mid, self.breadth - 1, 1)
        total = (
            self.coef(0, b) * above + self.coef(1, b) * below + self.coef(2, b) * sides
        )
        return mid, total

    def half(self, colour):
        chosen = self.parity() == float(colour)

        def body(b):
            mid, total = self.neighbours(b)
            updated = (self.g[pl.ds(b, self.n), :] + total) * self.coef(4, b)
            self.v[pl.ds(b + PAD, self.n), :] = jnp.where(chosen, updated, mid)

        self.loop(body)

    def sweeps(self, count):
        for _ in range(count):
            self.half(0)
            self.half(1)

    def sweeps_from_zero(self, count):
        red = self.parity() == 0.0

        def body(b):
            updated = self.g[pl.ds(b, self.n), :] * self.coef(4, b)
            self.v[pl.ds(b + PAD, self.n), :] = jnp.where(red, updated, 0.0)

        self.loop(body)
        self.half(1)
        self.sweeps(count - 1)

    def residual(self, out):
        def body(b):
            mid, total = self.neighbours(b)
            s = self.g[pl.ds(b, self.n), :] - (self.coef(3, b) * mid - total)
            out[pl.ds(b, self.n), :] = jnp.where(self.coef(4, b) != 0.0, s, 0.0)

        self.loop(body)

    def add(self, p):
        inside = wide(self.cf[pl.ds(4 * self.rows, self.rows), :], self.breadth) != 0.0
        at = pl.ds(PAD, self.rows)
        self.v[at, :] = self.v[at, :] + jnp.where(inside, p, 0.0)


def one(cond):
    return jnp.where(cond, 1.0, 0.0).astype(jnp.float32)


def restricted(s, halo, period):
    rows, breadth = s.shape
    shape = (rows // 2, rows)
    gap = iota(shape, 1) - 2 * iota(shape, 0)
    weights = jnp.where(
        jnp.logical_or(gap == 0, gap == 1),
        0.375,
        jnp.where(jnp.logical_or(gap == -1, gap == 2), 0.125, 0.0),
    ).astype(jnp.float32)
    t = dot(weights, s[...], 0)
    u = 0.5 * (
        pltpu.roll(t, 1, 1)
        + 3.0 * t
        + 3.0 * pltpu.roll(t, breadth - 1, 1)
        + pltpu.roll(t, breadth - 2, 1)
    )
    own = breadth - (LANES if halo else 0)
    tiles = []
    if own >= 2 * LANES:
        shape = (2 * LANES, LANES)
        pick = one(iota(shape, 0) == 2 * iota(shape, 1))
        for k in range(own // (2 * LANES)):
            tiles.append(dot(u[:, 2 * LANES * k : 2 * LANES * (k + 1)], pick, 1))
    else:
        shape = (LANES, LANES)
        pick = one(iota(shape, 0) == 2 * (iota(shape, 1) % (period // 2)))
        tiles.append(dot(u, pick, 1))
    if halo:
        shape = (LANES, LANES)
        j, i = iota(shape, 0), iota(shape, 1)
        right = jnp.logical_and(j == 2 * i, j < SIDE)
        left = jnp.logical_and(j == 2 * i - LANES, j >= SIDE)
        tiles.append(dot(u[:, own:], one(jnp.logical_or(right, left)), 1))
    return tiles[0] if len(tiles) == 1 else jnp.concatenate(tiles, axis=1)


def prolonged(e, rows, shift, halo, fine_period):
    breadth = e.shape[1]
    a = 0.75 * e + 0.25 * pltpu.roll(e, 1, 1)
    b = 0.75 * e + 0.25 * pltpu.roll(e, breadth - 1, 1)
    own = breadth - (LANES if halo else 0)
    tiles = []

    def pair(k):
        at = slice(LANES * k, LANES * (k + 1))
        return jnp.concatenate([a[:, at], b[:, at]], axis=1)

    if fine_period > LANES:
        shape = (2 * LANES, 2 * LANES)
        i, j = iota(shape, 0), iota(shape, 1)
        spread = one(j == jnp.where(i < LANES, 2 * i, 2 * (i - LANES) + 1))
        for k in range(own // LANES):
            tiles.append(dot(pair(k), spread, 1))
    else:
        shape = (2 * LANES, LANES)
        i, j = iota(shape, 0), iota(shape, 1) % fine_period
        spread = one(j == jnp.where(i < LANES, 2 * i, 2 * (i - LANES) + 1))
        tiles.append(dot(pair(0), spread, 1))
    if halo:
        shape = (2 * LANES, LANES)
        i, j = iota(shape, 0), iota(shape, 1)
        lane = i % LANES
        source = jnp.where(j < SIDE, j // 2, j // 2 + SIDE)
        spread = one(jnp.logical_and(lane == source, i // LANES == j % 2))
        tiles.append(dot(pair(own // LANES), spread, 1))
    p = tiles[0] if len(tiles) == 1 else jnp.concatenate(tiles, axis=1)
    shape = (rows, e.shape[0])
    i, c = iota(shape, 0), iota(shape, 1)
    near = i // 2 + shift
    far = near + jnp.where(i % 2 == 0, -1, 1)
    weights = jnp.where(c == near, 0.75, jnp.where(c == far, 0.25, 0.0)).astype(jnp.float32)
    return dot(weights, p, 0)


def down_kernel(height, total, spacings, place, v, hv, g, hg, top, bottom, htop, hbottom, *refs):
    outs, scratch = refs[: 2 * SPREAD + 1], refs[2 * SPREAD + 1 :]
    halo = UP << SPREAD
    breadth = v.shape[1]
    rows = height + 2 * halo
    vb, gb = scratch[0], scratch[1]
    at = pl.ds(PAD + halo, height)
    vb[at, pl.ds(0, breadth)] = v[...]
    vb[at, pl.ds(breadth, LANES)] = hv[...]
    for buf, take, shift in ((vb, 0, PAD), (gb, halo, 0)):
        for at, block, corner in ((0, top, htop), (halo + height, bottom, hbottom)):
            at = pl.ds(at + shift, halo)
            buf[at, pl.ds(0, breadth)] = block[pl.ds(take, halo), :]
            buf[at, pl.ds(breadth, LANES)] = corner[pl.ds(take, halo), :]
    at = pl.ds(halo, height)
    gb[at, pl.ds(0, breadth)] = g[...]
    gb[at, pl.ds(breadth, LANES)] = hg[...]
    for l in range(SPREAD):
        vb, gb, cf, s = scratch[4 * l : 4 * l + 4]
        edge = halo >> l
        own = height >> l
        level = Level(vb, gb, cf, spacings[l], total >> l, place[0] * own - edge)
        level.fill()
        if l == 0:
            level.sweeps(PRE)
        else:
            level.sweeps_from_zero(PRE)
        outs[2 * l][...] = vb[pl.ds(PAD + edge - UP, own + 2 * UP), :]
        outs[2 * l + 1][...] = gb[pl.ds(edge - UP, own + 2 * UP), :]
        level.residual(s)
        coarse = restricted(s, True, None)
        if l + 1 < SPREAD:
            scratch[4 * (l + 1) + 1][...] = coarse
        else:
            edge, own = edge // 2, own // 2
            outs[2 * SPREAD][...] = coarse[edge : edge + own, : outs[2 * SPREAD].shape[1]]


def up_kernel(height, total, spacings, sizes, place, gathered, *refs):
    ins, refs = refs[: 2 * SPREAD], refs[2 * SPREAD :]
    out_v, out_s, scratch = refs[0], refs[1], refs[2:]
    rads, angs = sizes
    whole = []
    for l in range(SPREAD, LEVELS):
        v, g, cf, s = scratch[4 * (l - SPREAD) : 4 * (l - SPREAD) + 4]
        whole.append((Level(v, g, cf, spacings[l], total >> l, 0), s))
    g = whole[0][0].g
    piece = gathered.shape[1:]
    for k, (r, a) in enumerate(gather_order(rads, angs)[1]):
        row = pl.multiple_of((place[0] ^ r) * piece[0], 8)
        col = pl.multiple_of((place[1] ^ a) * piece[1], LANES)
        g[pl.ds(row, piece[0]), pl.ds(col, piece[1])] = gathered[k]

    def period(l):
        return (piece[1] * angs) >> (l - SPREAD)

    for l in range(SPREAD, LEVELS):
        level, s = whole[l - SPREAD]
        level.fill()
        if l == LEVELS - 1:
            level.sweeps_from_zero(COARSE_SWEEPS)
        else:
            level.sweeps_from_zero(PRE)
            level.residual(s)
            whole[l + 1 - SPREAD][0].g[...] = restricted(s, False, period(l))
    for l in range(LEVELS - 2, SPREAD - 1, -1):
        level, s = whole[l - SPREAD]
        coarse = whole[l + 1 - SPREAD][0]
        e = coarse.v[pl.ds(PAD, coarse.rows), :]
        level.add(prolonged(e, level.rows, 0, False, period(l)))
        level.sweeps(POST)
    v = whole[0][0].v
    start = place[1] * piece[1]
    across = piece[1] * angs
    at = pl.ds(pl.multiple_of(place[0] * piece[0], 8), piece[0] + 2 * UP)
    after = pl.multiple_of(lax.rem(start + piece[1], across), LANES)
    before = pl.multiple_of(lax.rem(start + across - LANES, across), LANES)
    tile = (piece[0] + 2 * UP, LANES)
    halo = jnp.where(iota(tile, 1) < SIDE, v[at, pl.ds(after, LANES)], v[at, pl.ds(before, LANES)])
    own = v[at, pl.ds(pl.multiple_of(start, LANES), piece[1])]
    e = jnp.concatenate([own, halo], axis=1)
    base = 4 * (LEVELS - SPREAD)
    for l in range(SPREAD - 1, -1, -1):
        v, cf = scratch[base + 2 * l : base + 2 * l + 2]
        own = height >> l
        level = Level(v, ins[2 * l + 1], cf, spacings[l], total >> l, place[0] * own - UP)
        level.fill()
        v[pl.ds(PAD, level.rows), :] = ins[2 * l][...]
        level.add(prolonged(e, level.rows, UP // 2, True, 2 * LANES))
        level.sweeps(POST)
        e = v[pl.ds(PAD, level.rows), :]
    s = scratch[-1]
    level.residual(s)
    breadth = out_v.shape[1]
    out_v[...] = v[pl.ds(PAD + UP, height), pl.ds(0, breadth)]
    out_s[...] = s[pl.ds(UP, height), pl.ds(0, breadth)]


def gather_order(rads, angs):
    rounds = [("rad", 1 << k) for k in range(rads.bit_length() - 2, 0, -1)]
    rounds += [("ang", 1 << k) for k in range(angs.bit_length() - 1)]
    rounds += [("rad", 1)] if rads > 1 else []
    held = [(0, 0)]
    for axis, bit in rounds:
        held += [(r ^ bit, a) if axis == "rad" else (r, a ^ bit) for r, a in held]
    return rounds, held


def gather_pieces(piece, rads, angs):
    held = piece[None]
    for axis, bit in gather_order(rads, angs)[0]:
        pairs = [(i, i ^ bit) for i in range(lax.axis_size(axis))]
        held = jnp.concatenate([held, lax.ppermute(held, axis, pairs)], axis=0)
    return held


def f32(*shape):
    return jax.ShapeDtypeStruct(shape, jnp.float32)


def vmem(*shape):
    return pltpu.VMEM(shape, jnp.float32)


def local(right_side, guess):
    height, breadth = right_side.shape
    rads, angs = lax.axis_size("rad"), lax.axis_size("ang")
    total = height * rads
    spacings = [2.0 * math.pi / ((breadth * angs) >> l) for l in range(LEVELS)]
    halo = UP << SPREAD
    ring_up = [(i, (i + 1) % angs) for i in range(angs)]
    ring_down = [(j, i) for i, j in ring_up]
    up = [(i, i + 1) for i in range(rads - 1)]
    down = [(j, i) for i, j in up]

    def spread(x, y):
        last = jnp.concatenate([x[-halo:], y[-halo:]], axis=0)
        leading = jnp.concatenate([x[:halo], y[:halo]], axis=0)
        return lax.ppermute(last, "rad", up), lax.ppermute(leading, "rad", down)

    above, below = spread(guess, right_side)
    first = jnp.concatenate([guess[:, :SIDE], right_side[:, :SIDE]], axis=1)
    last = jnp.concatenate([guess[:, -SIDE:], right_side[:, -SIDE:]], axis=1)
    after = lax.ppermute(first, "ang", ring_down)
    before = lax.ppermute(last, "ang", ring_up)
    halo_v = jnp.concatenate([after[:, :SIDE], before[:, :SIDE]], axis=1)
    halo_g = jnp.concatenate([after[:, SIDE:], before[:, SIDE:]], axis=1)
    corner_above, corner_below = spread(halo_v, halo_g)
    place = jnp.stack([lax.axis_index("rad"), lax.axis_index("ang")]).astype(jnp.int32)
    smem = pl.BlockSpec(memory_space=pltpu.SMEM)
    full = pl.BlockSpec(memory_space=pltpu.VMEM)

    kept, scratch = [], []
    for l in range(SPREAD):
        rows, cols = height >> l, (breadth >> l) + LANES
        kept += [f32(rows + 2 * UP, cols)] * 2
        rows += 2 * (halo >> l)
        scratch += [vmem(rows + 2 * PAD, cols), vmem(rows, cols), vmem(5 * rows, LANES), vmem(rows, cols)]
    piece = (height >> SPREAD, breadth >> SPREAD)
    *kept, coarse = pl.pallas_call(
        lambda *refs: down_kernel(height, total, spacings, *refs),
        out_shape=kept + [f32(*piece)],
        in_specs=[smem] + [full] * 8,
        out_specs=[full] * (2 * SPREAD + 1),
        scratch_shapes=scratch,
        compiler_params=pltpu.CompilerParams(vmem_limit_bytes=50 * 1024 * 1024),
        name="down",
    )(place, guess, halo_v, right_side, halo_g, above, below, corner_above, corner_below)

    gathered = gather_pieces(coarse, rads, angs)
    scratch = []
    for l in range(SPREAD, LEVELS):
        rows, cols = total >> l, max(LANES, (breadth * angs) >> l)
        scratch += [vmem(rows + 2 * PAD, cols), vmem(rows, cols), vmem(5 * rows, LANES), vmem(rows, cols)]
    for l in range(SPREAD):
        rows, cols = (height >> l) + 2 * UP, (breadth >> l) + LANES
        scratch += [vmem(rows + 2 * PAD, cols), vmem(5 * rows, LANES)]
    scratch.append(vmem(height + 2 * UP, breadth + LANES))
    return tuple(
        pl.pallas_call(
            lambda *refs: up_kernel(height, total, spacings, (rads, angs), *refs),
            out_shape=[f32(height, breadth)] * 2,
            in_specs=[smem] + [full] * (2 * SPREAD + 1),
            out_specs=[full] * 2,
            scratch_shapes=scratch,
            compiler_params=pltpu.CompilerParams(vmem_limit_bytes=50 * 1024 * 1024),
            name="up",
        )(place, gathered, *kept)
    )


def solution(mesh):
    placed = (P("rad", "ang"), P("rad", "ang"))
    return jax.shard_map(
        local,
        mesh=mesh,
        in_specs=placed,
        out_specs=(P("rad", "ang"), P("rad", "ang")),
        check_vma=False,
    )
```

```python
import math

import jax
import jax.numpy as jnp
from jax import lax
from jax.experimental import pallas as pl
from jax.experimental.pallas import tpu as pltpu
from jax.sharding import PartitionSpec as P

LEVELS = 8
PRE = 2
POST = 2
COARSE_SWEEPS = 8
SPREAD = 3
PAD = 8
UP = 8
LANES = 128
SIDE = 64


def iota(shape, dim):
    return lax.broadcasted_iota(jnp.int32, shape, dim)


def thirds(x):
    high = x.astype(jnp.bfloat16)
    rest = x - high.astype(jnp.float32)
    middle = rest.astype(jnp.bfloat16)
    return high, middle, (rest - middle.astype(jnp.float32)).astype(jnp.bfloat16)


def product(a, b):
    return lax.dot_general(a, b, (((1,), (0,)), ((), ())), preferred_element_type=jnp.float32)


def dot(a, b, exact):
    if exact == 0:
        a = a.astype(jnp.bfloat16)
        high, middle, low = [product(a, x) for x in thirds(b)]
    else:
        b = b.astype(jnp.bfloat16)
        high, middle, low = [product(x, b) for x in thirds(a)]
    return high + (middle + low)


def wide(x, breadth):
    return x if breadth == LANES else jnp.concatenate([x] * (breadth // LANES), axis=1)


def chunk_of(rows, breadth):
    units = rows // 8
    best = 1
    for n in range(1, units + 1):
        if units % n == 0 and n * 8 * breadth <= 80 * 1024:
            best = n
    return 8 * best


class Level:
    def __init__(self, v, g, cf, spacing, total, first):
        self.v, self.g, self.cf = v, g, cf
        self.rows, self.breadth = g.shape
        self.spacing, self.total, self.first = spacing, total, first
        self.n = chunk_of(self.rows, self.breadth)

    def fill(self):
        shape = (self.rows, LANES)
        ids = self.first + iota(shape, 0)
        radius = 1.0 + (ids.astype(jnp.float32) + 0.5) * self.spacing
        ratio = 0.5 * self.spacing / radius
        angular = 1.0 / (radius * radius)
        centre = 2.0 + 2.0 * angular
        inside = jnp.logical_and(ids >= 0, ids < self.total)
        self.cf[pl.ds(0 * self.rows, self.rows), :] = 1.0 + ratio
        self.cf[pl.ds(1 * self.rows, self.rows), :] = 1.0 - ratio
        self.cf[pl.ds(2 * self.rows, self.rows), :] = angular
        self.cf[pl.ds(3 * self.rows, self.rows), :] = centre
        self.cf[pl.ds(4 * self.rows, self.rows), :] = jnp.where(inside, 1.0 / centre, 0.0)
        zero = jnp.zeros((PAD, self.breadth), jnp.float32)
        self.v[pl.ds(0, PAD), :] = zero
        self.v[pl.ds(PAD + self.rows, PAD), :] = zero

    def loop(self, body):
        steps = self.rows // self.n
        if steps == 1:
            body(0)
        else:
            def step(k, carry):
                body(pl.multiple_of(k * self.n, 8))
                return carry

            lax.fori_loop(0, steps, step, 0)

    def coef(self, which, b):
        return wide(self.cf[pl.ds(which * self.rows + b, self.n), :], self.breadth)

    def parity(self):
        shape = (self.n, LANES)
        return wide(((iota(shape, 0) + iota(shape, 1)) & 1).astype(jnp.float32), self.breadth)

    def neighbours(self, b):
        near = self.v[pl.ds(b, self.n + 2 * PAD), :]
        mid = near[PAD : PAD + self.n]
        below = near[PAD - 1 : PAD - 1 + self.n]
        above = near[PAD + 1 : PAD + 1 + self.n]
        sides = pltpu.roll(mid, 1, 1) + pltpu.roll(mid, self.breadth - 1, 1)
        total = (
            self.coef(0, b) * above + self.coef(1, b) * below + self.coef(2, b) * sides
        )
        return mid, total

    def half(self, colour):
        chosen = self.parity() == float(colour)

        def body(b):
            mid, total = self.neighbours(b)
            updated = (self.g[pl.ds(b, self.n), :] + total) * self.coef(4, b)
            self.v[pl.ds(b + PAD, self.n), :] = jnp.where(chosen, updated, mid)

        self.loop(body)

    def sweeps(self, count):
        for _ in range(count):
            self.half(0)
            self.half(1)

    def sweeps_from_zero(self, count):
        red = self.parity() == 0.0

        def body(b):
            updated = self.g[pl.ds(b, self.n), :] * self.coef(4, b)
            self.v[pl.ds(b + PAD, self.n), :] = jnp.where(red, updated, 0.0)

        self.loop(body)
        self.half(1)
        self.sweeps(count - 1)

    def residual(self, out):
        def body(b):
            mid, total = self.neighbours(b)
            s = self.g[pl.ds(b, self.n), :] - (self.coef(3, b) * mid - total)
            out[pl.ds(b, self.n), :] = jnp.where(self.coef(4, b) != 0.0, s, 0.0)

        self.loop(body)

    def add(self, p):
        inside = wide(self.cf[pl.ds(4 * self.rows, self.rows), :], self.breadth) != 0.0
        at = pl.ds(PAD, self.rows)
        self.v[at, :] = self.v[at, :] + jnp.where(inside, p, 0.0)


def one(cond):
    return jnp.where(cond, 1.0, 0.0).astype(jnp.float32)


def restricted(s, halo, period):
    rows, breadth = s.shape
    shape = (rows // 2, rows)
    gap = iota(shape, 1) - 2 * iota(shape, 0)
    weights = jnp.where(
        jnp.logical_or(gap == 0, gap == 1),
        0.375,
        jnp.where(jnp.logical_or(gap == -1, gap == 2), 0.125, 0.0),
    ).astype(jnp.float32)
    t = dot(weights, s[...], 0)
    u = 0.5 * (
        pltpu.roll(t, 1, 1)
        + 3.0 * t
        + 3.0 * pltpu.roll(t, breadth - 1, 1)
        + pltpu.roll(t, breadth - 2, 1)
    )
    own = breadth - (LANES if halo else 0)
    tiles = []
    if own >= 2 * LANES:
        shape = (2 * LANES, LANES)
        pick = one(iota(shape, 0) == 2 * iota(shape, 1))
        for k in range(own // (2 * LANES)):
            tiles.append(dot(u[:, 2 * LANES * k : 2 * LANES * (k + 1)], pick, 1))
    else:
        shape = (LANES, LANES)
        pick = one(iota(shape, 0) == 2 * (iota(shape, 1) % (period // 2)))
        tiles.append(dot(u, pick, 1))
    if halo:
        shape = (LANES, LANES)
        j, i = iota(shape, 0), iota(shape, 1)
        right = jnp.logical_and(j == 2 * i, j < SIDE)
        left = jnp.logical_and(j == 2 * i - LANES, j >= SIDE)
        tiles.append(dot(u[:, own:], one(jnp.logical_or(right, left)), 1))
    return tiles[0] if len(tiles) == 1 else jnp.concatenate(tiles, axis=1)


def prolonged(e, rows, shift, halo, fine_period):
    breadth = e.shape[1]
    a = 0.75 * e + 0.25 * pltpu.roll(e, 1, 1)
    b = 0.75 * e + 0.25 * pltpu.roll(e, breadth - 1, 1)
    own = breadth - (LANES if halo else 0)
    tiles = []

    def pair(k):
        at = slice(LANES * k, LANES * (k + 1))
        return jnp.concatenate([a[:, at], b[:, at]], axis=1)

    if fine_period > LANES:
        shape = (2 * LANES, 2 * LANES)
        i, j = iota(shape, 0), iota(shape, 1)
        spread = one(j == jnp.where(i < LANES, 2 * i, 2 * (i - LANES) + 1))
        for k in range(own // LANES):
            tiles.append(dot(pair(k), spread, 1))
    else:
        shape = (2 * LANES, LANES)
        i, j = iota(shape, 0), iota(shape, 1) % fine_period
        spread = one(j == jnp.where(i < LANES, 2 * i, 2 * (i - LANES) + 1))
        tiles.append(dot(pair(0), spread, 1))
    if halo:
        shape = (2 * LANES, LANES)
        i, j = iota(shape, 0), iota(shape, 1)
        lane = i % LANES
        source = jnp.where(j < SIDE, j // 2, j // 2 + SIDE)
        spread = one(jnp.logical_and(lane == source, i // LANES == j % 2))
        tiles.append(dot(pair(own // LANES), spread, 1))
    p = tiles[0] if len(tiles) == 1 else jnp.concatenate(tiles, axis=1)
    shape = (rows, e.shape[0])
    i, c = iota(shape, 0), iota(shape, 1)
    near = i // 2 + shift
    far = near + jnp.where(i % 2 == 0, -1, 1)
    weights = jnp.where(c == near, 0.75, jnp.where(c == far, 0.25, 0.0)).astype(jnp.float32)
    return dot(weights, p, 0)


def down_kernel(height, total, spacings, place, v, hv, g, hg, top, bottom, htop, hbottom, *refs):
    outs, scratch = refs[: 2 * SPREAD + 1], refs[2 * SPREAD + 1 :]
    halo = UP << SPREAD
    breadth = v.shape[1]
    rows = height + 2 * halo
    vb, gb = scratch[0], scratch[1]
    at = pl.ds(PAD + halo, height)
    vb[at, pl.ds(0, breadth)] = v[...]
    vb[at, pl.ds(breadth, LANES)] = hv[...]
    for buf, take, shift in ((vb, 0, PAD), (gb, halo, 0)):
        for at, block, corner in ((0, top, htop), (halo + height, bottom, hbottom)):
            at = pl.ds(at + shift, halo)
            buf[at, pl.ds(0, breadth)] = block[pl.ds(take, halo), :]
            buf[at, pl.ds(breadth, LANES)] = corner[pl.ds(take, halo), :]
    at = pl.ds(halo, height)
    gb[at, pl.ds(0, breadth)] = g[...]
    gb[at, pl.ds(breadth, LANES)] = hg[...]
    for l in range(SPREAD):
        vb, gb, cf, s = scratch[4 * l : 4 * l + 4]
        edge = halo >> l
        own = height >> l
        level = Level(vb, gb, cf, spacings[l], total >> l, place[0] * own - edge)
        level.fill()
        if l == 0:
            level.sweeps(PRE)
        else:
            level.sweeps_from_zero(PRE)
        outs[2 * l][...] = vb[pl.ds(PAD + edge - UP, own + 2 * UP), :]
        outs[2 * l + 1][...] = gb[pl.ds(edge - UP, own + 2 * UP), :]
        level.residual(s)
        coarse = restricted(s, True, None)
        if l + 1 < SPREAD:
            scratch[4 * (l + 1) + 1][...] = coarse
        else:
            edge, own = edge // 2, own // 2
            outs[2 * SPREAD][...] = coarse[edge : edge + own, : outs[2 * SPREAD].shape[1]]


def up_kernel(height, total, spacings, sizes, place, gathered, *refs):
    ins, refs = refs[: 2 * SPREAD], refs[2 * SPREAD :]
    out_v, out_s, scratch = refs[0], refs[1], refs[2:]
    rads, angs = sizes
    whole = []
    for l in range(SPREAD, LEVELS):
        v, g, cf, s = scratch[4 * (l - SPREAD) : 4 * (l - SPREAD) + 4]
        whole.append((Level(v, g, cf, spacings[l], total >> l, 0), s))
    g = whole[0][0].g
    piece = gathered.shape[1:]
    for k, (r, a) in enumerate(gather_order(rads, angs)[1]):
        row = pl.multiple_of((place[0] ^ r) * piece[0], 8)
        col = pl.multiple_of((place[1] ^ a) * piece[1], LANES)
        g[pl.ds(row, piece[0]), pl.ds(col, piece[1])] = gathered[k]

    def period(l):
        return (piece[1] * angs) >> (l - SPREAD)

    for l in range(SPREAD, LEVELS):
        level, s = whole[l - SPREAD]
        level.fill()
        if l == LEVELS - 1:
            level.sweeps_from_zero(COARSE_SWEEPS)
        else:
            level.sweeps_from_zero(PRE)
            level.residual(s)
            whole[l + 1 - SPREAD][0].g[...] = restricted(s, False, period(l))
    for l in range(LEVELS - 2, SPREAD - 1, -1):
        level, s = whole[l - SPREAD]
        coarse = whole[l + 1 - SPREAD][0]
        e = coarse.v[pl.ds(PAD, coarse.rows), :]
        level.add(prolonged(e, level.rows, 0, False, period(l)))
        level.sweeps(POST)
    v = whole[0][0].v
    start = place[1] * piece[1]
    across = piece[1] * angs
    at = pl.ds(pl.multiple_of(place[0] * piece[0], 8), piece[0] + 2 * UP)
    after = pl.multiple_of(lax.rem(start + piece[1], across), LANES)
    before = pl.multiple_of(lax.rem(start + across - LANES, across), LANES)
    tile = (piece[0] + 2 * UP, LANES)
    halo = jnp.where(iota(tile, 1) < SIDE, v[at, pl.ds(after, LANES)], v[at, pl.ds(before, LANES)])
    own = v[at, pl.ds(pl.multiple_of(start, LANES), piece[1])]
    e = jnp.concatenate([own, halo], axis=1)
    base = 4 * (LEVELS - SPREAD)
    for l in range(SPREAD - 1, -1, -1):
        v, cf = scratch[base + 2 * l : base + 2 * l + 2]
        own = height >> l
        level = Level(v, ins[2 * l + 1], cf, spacings[l], total >> l, place[0] * own - UP)
        level.fill()
        v[pl.ds(PAD, level.rows), :] = ins[2 * l][...]
        level.add(prolonged(e, level.rows, UP // 2, True, 2 * LANES))
        level.sweeps(POST)
        e = v[pl.ds(PAD, level.rows), :]
    s = scratch[-1]
    level.residual(s)
    breadth = out_v.shape[1]
    out_v[...] = v[pl.ds(PAD + UP, height), pl.ds(0, breadth)]
    out_s[...] = s[pl.ds(UP, height), pl.ds(0, breadth)]


def gather_order(rads, angs):
    rounds = [("rad", 1 << k) for k in range(rads.bit_length() - 2, 0, -1)]
    rounds += [("ang", 1 << k) for k in range(angs.bit_length() - 1)]
    rounds += [("rad", 1)] if rads > 1 else []
    held = [(0, 0)]
    for axis, bit in rounds:
        held += [(r ^ bit, a) if axis == "rad" else (r, a ^ bit) for r, a in held]
    return rounds, held


def gather_pieces(piece, rads, angs):
    held = piece[None]
    for axis, bit in gather_order(rads, angs)[0]:
        pairs = [(i, i ^ bit) for i in range(lax.axis_size(axis))]
        held = jnp.concatenate([held, lax.ppermute(held, axis, pairs)], axis=0)
    return held


def f32(*shape):
    return jax.ShapeDtypeStruct(shape, jnp.float32)


def vmem(*shape):
    return pltpu.VMEM(shape, jnp.float32)


def local(right_side, guess):
    height, breadth = right_side.shape
    rads, angs = lax.axis_size("rad"), lax.axis_size("ang")
    total = height * rads
    spacings = [2.0 * math.pi / ((breadth * angs) >> l) for l in range(LEVELS)]
    halo = UP << SPREAD
    ring_up = [(i, (i + 1) % angs) for i in range(angs)]
    ring_down = [(j, i) for i, j in ring_up]
    up = [(i, i + 1) for i in range(rads - 1)]
    down = [(j, i) for i, j in up]

    def spread(x, y):
        last = jnp.concatenate([x[-halo:], y[-halo:]], axis=0)
        leading = jnp.concatenate([x[:halo], y[:halo]], axis=0)
        return lax.ppermute(last, "rad", up), lax.ppermute(leading, "rad", down)

    above, below = spread(guess, right_side)
    first = jnp.concatenate([guess[:, :SIDE], right_side[:, :SIDE]], axis=1)
    last = jnp.concatenate([guess[:, -SIDE:], right_side[:, -SIDE:]], axis=1)
    after = lax.ppermute(first, "ang", ring_down)
    before = lax.ppermute(last, "ang", ring_up)
    halo_v = jnp.concatenate([after[:, :SIDE], before[:, :SIDE]], axis=1)
    halo_g = jnp.concatenate([after[:, SIDE:], before[:, SIDE:]], axis=1)

    def corner(strip_first, strip_last, step):
        rows = range(rads - 1) if step > 0 else range(1, rads)
        moves = [(r, (a + 1) % angs, a) for r in rows for a in range(angs)]
        from_after = [(b * rads + r, a * rads + r + step) for r, b, a in moves]
        from_before = [(a * rads + r, b * rads + r + step) for r, b, a in moves]
        right = lax.ppermute(strip_first, ("ang", "rad"), from_after)
        left = lax.ppermute(strip_last, ("ang", "rad"), from_before)
        top = jnp.concatenate([right[:, :SIDE], left[:, :SIDE]], axis=1)
        low = jnp.concatenate([right[:, SIDE:], left[:, SIDE:]], axis=1)
        return jnp.concatenate([top, low], axis=0)

    corner_above = corner(first[-halo:], last[-halo:], 1)
    corner_below = corner(first[:halo], last[:halo], -1)
    place = jnp.stack([lax.axis_index("rad"), lax.axis_index("ang")]).astype(jnp.int32)
    smem = pl.BlockSpec(memory_space=pltpu.SMEM)
    full = pl.BlockSpec(memory_space=pltpu.VMEM)

    kept, scratch = [], []
    for l in range(SPREAD):
        rows, cols = height >> l, (breadth >> l) + LANES
        kept += [f32(rows + 2 * UP, cols)] * 2
        rows += 2 * (halo >> l)
        scratch += [vmem(rows + 2 * PAD, cols), vmem(rows, cols), vmem(5 * rows, LANES), vmem(rows, cols)]
    piece = (height >> SPREAD, breadth >> SPREAD)
    *kept, coarse = pl.pallas_call(
        lambda *refs: down_kernel(height, total, spacings, *refs),
        out_shape=kept + [f32(*piece)],
        in_specs=[smem] + [full] * 8,
        out_specs=[full] * (2 * SPREAD + 1),
        scratch_shapes=scratch,
        compiler_params=pltpu.CompilerParams(vmem_limit_bytes=50 * 1024 * 1024),
        name="down",
    )(place, guess, halo_v, right_side, halo_g, above, below, corner_above, corner_below)

    gathered = gather_pieces(coarse, rads, angs)
    scratch = []
    for l in range(SPREAD, LEVELS):
        rows, cols = total >> l, max(LANES, (breadth * angs) >> l)
        scratch += [vmem(rows + 2 * PAD, cols), vmem(rows, cols), vmem(5 * rows, LANES), vmem(rows, cols)]
    for l in range(SPREAD):
        rows, cols = (height >> l) + 2 * UP, (breadth >> l) + LANES
        scratch += [vmem(rows + 2 * PAD, cols), vmem(5 * rows, LANES)]
    scratch.append(vmem(height + 2 * UP, breadth + LANES))
    return tuple(
        pl.pallas_call(
            lambda *refs: up_kernel(height, total, spacings, (rads, angs), *refs),
            out_shape=[f32(height, breadth)] * 2,
            in_specs=[smem] + [full] * (2 * SPREAD + 1),
            out_specs=[full] * 2,
            scratch_shapes=scratch,
            compiler_params=pltpu.CompilerParams(vmem_limit_bytes=50 * 1024 * 1024),
            name="up",
        )(place, gathered, *kept)
    )


def solution(mesh):
    placed = (P("rad", "ang"), P("rad", "ang"))
    return jax.shard_map(
        local,
        mesh=mesh,
        in_specs=placed,
        out_specs=(P("rad", "ang"), P("rad", "ang")),
        check_vma=False,
    )
```
